32 devices in a mesh: rows: 8 (over z, y), grp: 4 (over x, core).
Axes of the slice: x: 2, y: 2, z: 4, core: 2. Of those that a mesh axis runs over, the one named last changes fastest.
Arguments:
- mat: float32 [16384, 1024], P(('rows', 'grp'))
- signs: int32 [16384], P(('rows', 'grp')), may hold values from -1 to 1, as said below
- picks: int32 [2048], P(('rows', 'grp')), may hold values from 0 to 16383, as said below
- rhs: float32 [16384, 128], P(('rows', 'grp'))
Outputs:
- tri: float32 [1024, 1024], replicated
- solution: float32 [1024, 128], replicated
- residual: float32 [16384, 128], P(('rows', 'grp'))
The draws below stay inside these ranges and needn't reach their ends.
Inputs may be any that keep to these rules, and one draw needn't show every extreme that they name: `signs`: every entry is -1 or 1. `picks`: the entries k * 64 to (k + 1) * 64 - 1 are distinct row indices in k * 512 to (k + 1) * 512 - 1.
All inputs are finite; a program needn't handle non-finite values.
Results may differ from the reference program's by a relative error of at most 0.000088.
Values sent between devices are 32-bit elements; how exact they have to be, the bound alone decides.
A program may use at most 64 MiB of HBM per device.

```python
import math
import jax
import jax.numpy as jnp
from jax import lax

N = 1024
L = 512
SAMP_DEV = 64
K = 128
M = 16384


def row_profile(key, rough_low, rough_high):
    ramp = 1.0 + 2.0 * jnp.arange(M, dtype=jnp.float32) / max(M - 1, 1)
    rough = jnp.exp(jax.random.uniform(key, (M,), jnp.float32, math.log(rough_low), math.log(rough_high)))
    return ramp * rough


def draw_mat(key, part):
    entries = jax.random.normal(jax.random.fold_in(key, 1), (M, N), jnp.float32)
    col_scale = jnp.exp(jax.random.uniform(jax.random.fold_in(key, 2), (N,), jnp.float32, 0.0, math.log(10.0)))
    row_scale = row_profile(jax.random.fold_in(key, 3), 0.7, 1.4)
    return (entries * col_scale[None, :] * row_scale[:, None] / math.sqrt(M)).astype(jnp.float32)


def draw_rhs(key, part):
    entries = jax.random.normal(jax.random.fold_in(key, 21), (M, K), jnp.float32)
    row_scale = row_profile(jax.random.fold_in(key, 23), 0.7, 1.4)
    return (entries * row_scale[:, None]).astype(jnp.float32)


def draw_signs(key, part):
    coins = jax.random.randint(jax.random.fold_in(key, 31), (M,), 0, 2)
    return (2 * coins - 1).astype(jnp.int32)


def draw_picks(key, part):
    block_count = M // L
    block_keys = jax.random.split(jax.random.fold_in(key, 41), block_count)
    block_ids = jnp.arange(block_count, dtype=jnp.int32)
    free_value = jax.random.randint(jax.random.fold_in(key, 42), (block_count,), 0, L).astype(jnp.int32)
    forced = jnp.where(block_ids == block_count - 1, L - 1, free_value)
    forced = jnp.where(block_ids == 0, 0, forced).astype(jnp.int32)

    def one_block(block_key, fixed_value):
        others = jax.random.permutation(block_key, L - 1)[:SAMP_DEV - 1].astype(jnp.int32)
        others = others + (others >= fixed_value).astype(jnp.int32)
        return jnp.concatenate([fixed_value[None], others])
    offsets = jax.vmap(one_block)(block_keys, forced)
    return (block_ids[:, None] * L + offsets).reshape(-1).astype(jnp.int32)


def setup_inputs(seed: int = 0) -> dict:
    seeds = jax.random.split(jax.random.key(seed), 5)
    mat = draw_mat(jax.random.fold_in(seeds[4], 71), 0)
    signs = draw_signs(jax.random.fold_in(seeds[4], 71), 0)
    picks = draw_picks(jax.random.fold_in(seeds[4], 71), 0)
    rhs = draw_rhs(jax.random.fold_in(seeds[4], 71), 0)
    return dict(mat=mat, signs=signs, picks=picks, rhs=rhs)


def walsh_rows(columns):
    total = columns.shape[0]
    col_count = columns.shape[1]
    half_span = 1
    while half_span < total:
        paired = columns.reshape(total // (2 * half_span), 2, half_span, col_count)
        upper_half = paired[:, 0] + paired[:, 1]
        lower_half = paired[:, 0] - paired[:, 1]
        columns = jnp.stack([upper_half, lower_half], axis=1).reshape(total, col_count)
        half_span = half_span * 2
    return columns

def reference(mat, signs, picks, rhs):
    total = mat.shape[0]
    samples = picks.shape[0]
    signed = mat * signs.astype(jnp.float32)[:, None]
    block_width = min(128, N)
    stacked = signed.reshape(total, N // block_width, block_width).transpose(1, 0, 2)

    def sketch_block(columns):
        return walsh_rows(columns)[picks]
    picked = lax.map(sketch_block, stacked)
    sketch = picked.transpose(1, 0, 2).reshape(samples, N) * (1.0 / math.sqrt(samples))
    gram = jnp.dot(sketch.T, sketch, precision=lax.Precision.HIGHEST)
    lower = jnp.linalg.cholesky(gram)
    beta = jnp.sqrt(lax.optimization_barrier(jnp.sum(rhs * rhs, axis=0)))
    atb = jnp.dot(mat.T, rhs, precision=lax.Precision.HIGHEST)
    lifted = lax.linalg.triangular_solve(lower, atb, left_side=True, lower=True) / beta
    alpha = jnp.sqrt(lax.optimization_barrier(jnp.sum(lifted * lifted, axis=0)))
    unit = lifted / alpha
    direction = lax.linalg.triangular_solve(lower, unit, left_side=True, lower=True, transpose_a=True)
    image = jnp.dot(mat, direction, precision=lax.Precision.HIGHEST)
    pushed = image - alpha / beta * rhs
    gamma = jnp.sqrt(lax.optimization_barrier(jnp.sum(pushed * pushed, axis=0)))
    coef = beta * alpha / (alpha * alpha + gamma * gamma)
    return (lower.T, direction * coef, rhs - image * coef)
```

```python
import functools

import jax
import jax.numpy as jnp
from jax import lax
from jax.experimental import pallas as pl
from jax.experimental.pallas import tpu as pltpu
from jax.sharding import PartitionSpec as P

exact_mode = lax.Precision.HIGHEST
TILE = 128
SUB = 8
AXES = ("rows", "grp")


def walsh_table(table_order, piece=1):
    counter = lax.iota(jnp.int32, table_order)
    outer = counter // piece
    common_bits = outer[:, None] & outer[None, :]
    parity = jnp.zeros((table_order, table_order), jnp.int32)
    for bit_pos in range(max((table_order // piece).bit_length() - 1, 0)):
        parity = parity + (common_bits >> bit_pos & 1)
    table = jnp.where(parity % 2 == 0, 1.0, -1.0).astype(jnp.float32)
    inner = counter % piece
    return jnp.where(inner[:, None] == inner[None, :], table, 0.0)


def dot_tt(a, b):
    return lax.dot_general(a, b, (((0,), (0,)), ((), ())), precision=exact_mode,
                           preferred_element_type=jnp.float32)


def dot_nn(a, b):
    return lax.dot_general(a, b, (((1,), (0,)), ((), ())), precision=exact_mode,
                           preferred_element_type=jnp.float32)


def factor_tile(block):
    groups = TILE // SUB
    lane = lax.broadcasted_iota(jnp.int32, (SUB, TILE), 1)
    sub = lax.broadcasted_iota(jnp.int32, (SUB, TILE), 0)
    left = [block[SUB * g:SUB * (g + 1), :] for g in range(groups)]
    right = [(lane == sub + SUB * g).astype(jnp.float32) for g in range(groups)]
    for j in range(TILE):
        g, s = divmod(j, SUB)
        inv = 1.0 / left[g][s:s + 1, j:j + 1]
        row = left[g][s:s + 1, :] * inv
        row_e = right[g][s:s + 1, :] * inv
        for h in range(g, groups):
            col = jnp.broadcast_to(left[h][:, j:j + 1], (SUB, TILE))
            if h == g:
                if s == SUB - 1:
                    continue
                col = jnp.where(sub > s, col, 0.0)
            left[h] = left[h] - col * row
            right[h] = right[h] - col * row_e
    for g in range(groups):
        pivot = jnp.sum(jnp.where(lane == sub + SUB * g, left[g], 0.0), axis=1, keepdims=True)
        root = jnp.sqrt(pivot)
        left[g] = jnp.where(lane >= sub + SUB * g, left[g] / root, 0.0)
        right[g] = jnp.where(lane <= sub + SUB * g, right[g] / root, 0.0)
    return jnp.concatenate(left, axis=0), jnp.concatenate(right, axis=0)


def factor_kernel(packed_ref, atb_ref, squares_ref, tri_ref, direction_ref, alpha_ref, work, inverse):
    n = tri_ref.shape[0]
    tiles = n // TILE
    offset = 0
    for i in range(tiles):
        width = n - i * TILE
        work[i * TILE:(i + 1) * TILE, i * TILE:n] = packed_ref[:, offset:offset + width]
        if i:
            work[i * TILE:(i + 1) * TILE, :i * TILE] = jnp.zeros((TILE, i * TILE), jnp.float32)
        offset += width
    work[:, n:] = atb_ref[...]
    width = work.shape[1]

    def step(k, carry):
        at = pl.multiple_of(k * TILE, TILE)
        here = pl.ds(at, TILE)
        upper, inv = factor_tile(work[here, here])
        inverse[here, :] = inv
        column = lax.broadcasted_iota(jnp.int32, (TILE, width), 1)
        panel = dot_nn(inv, work[here, :])
        work[here, :] = jnp.where(column >= at + TILE, panel, 0.0)
        work[here, here] = upper

        def trail(i, carry):
            there = pl.ds(pl.multiple_of(i * TILE, TILE), TILE)
            work[there, :] = work[there, :] - dot_tt(work[here, there], work[here, :])
            return carry

        return lax.fori_loop(k + 1, tiles, trail, carry)

    lax.fori_loop(0, tiles, step, 0)
    tri_ref[...] = work[:, :n]
    beta = jnp.sqrt(squares_ref[0:1, :])
    lifted = work[:, n:] / beta
    alpha = jnp.sqrt(jnp.sum(lifted * lifted, axis=0, keepdims=True))
    alpha_ref[...] = jnp.broadcast_to(alpha, alpha_ref.shape)
    work[:, n:] = lifted / alpha
    direction_ref[...] = jnp.zeros_like(direction_ref)

    def back(t, carry):
        k = tiles - 1 - t
        here = pl.ds(pl.multiple_of(k * TILE, TILE), TILE)
        rest = work[here, n:] - dot_nn(tri_ref[here, :], direction_ref[...])
        direction_ref[here, :] = dot_tt(inverse[here, :], rest)
        return carry

    lax.fori_loop(0, tiles, back, 0)


def factor_and_solve(packed, atb, squares):
    n, k = atb.shape
    return pl.pallas_call(
        factor_kernel,
        out_shape=(
            jax.ShapeDtypeStruct((n, n), jnp.float32),
            jax.ShapeDtypeStruct((n, k), jnp.float32),
            jax.ShapeDtypeStruct((SUB, k), jnp.float32),
        ),
        in_specs=[pl.BlockSpec(memory_space=pltpu.VMEM)] * 3,
        out_specs=(pl.BlockSpec(memory_space=pltpu.VMEM),) * 3,
        scratch_shapes=[
            pltpu.VMEM((n, n + k), jnp.float32),
            pltpu.VMEM((n, TILE), jnp.float32),
        ],
        compiler_params=pltpu.CompilerParams(vmem_limit_bytes=48 * 1024 * 1024),
        name="factor_and_solve",
    )(packed, atb, squares)


def shards(mat, signs, picks, rhs):
    row_count, n = mat.shape
    devices = lax.axis_size("rows") * lax.axis_size("grp")
    samples = picks.shape[0] * devices
    piece = row_count // devices

    atb_part = dot_tt(mat, rhs)
    squares_part = jnp.sum(rhs * rhs, axis=0, keepdims=True)
    squares_part = jnp.concatenate(
        [squares_part, jnp.zeros((SUB - 1, rhs.shape[1]), jnp.float32)], axis=0
    )
    early = lax.psum(jnp.concatenate([atb_part, squares_part], axis=0), AXES)
    atb, squares = early[:n], early[n:]

    local_rows = lax.iota(jnp.int32, row_count)
    hits = jnp.sum(
        ((picks % row_count)[:, None] == local_rows[None, :]).astype(jnp.float32), axis=0
    ) * (1.0 / samples)
    hits = lax.all_to_all(hits.reshape(devices, piece), AXES, 0, 0, tiled=True)

    mixed = mat * signs.astype(jnp.float32)[:, None]
    mixed = dot_nn(walsh_table(row_count), mixed)
    if piece % SUB == 0:
        turned = lax.all_to_all(mixed, AXES, 0, 0, tiled=True)
    else:
        turned = mixed.reshape(devices, piece * n // TILE, TILE)
        turned = lax.all_to_all(turned, AXES, 0, 0, tiled=True).reshape(row_count, n)
    turned = dot_nn(walsh_table(row_count, piece), turned)
    weighted = turned * hits.reshape(row_count, 1)
    strips = [
        dot_tt(weighted[:, at:at + TILE], turned[:, at:]) for at in range(0, n, TILE)
    ]
    packed = lax.psum(jnp.concatenate(strips, axis=1), AXES)

    tri, direction, alpha = factor_and_solve(packed, atb, squares)
    alpha = alpha[0]
    beta = jnp.sqrt(squares[0])
    image = dot_nn(mat, direction)
    pushed = image - alpha / beta * rhs
    gamma_sq = lax.psum(jnp.sum(pushed * pushed, axis=0), AXES)
    coef = beta * alpha / (alpha * alpha + gamma_sq)
    return (tri, direction * coef, rhs - image * coef)


def solution(mesh):
    return jax.shard_map(
        shards,
        mesh=mesh,
        in_specs=(P(AXES, None), P(AXES), P(AXES), P(AXES, None)),
        out_specs=(P(), P(), P(AXES, None)),
        check_vma=False,
    )
```

```python
import functools

import jax
import jax.numpy as jnp
from jax import lax
from jax.experimental import pallas as pl
from jax.experimental.pallas import tpu as pltpu
from jax.sharding import PartitionSpec as P

exact_mode = lax.Precision.HIGHEST
TILE = 128
SUB = 8
AXES = ("rows", "grp")


def walsh_table(table_order, piece=1):
    counter = lax.iota(jnp.int32, table_order)
    outer = counter // piece
    common_bits = outer[:, None] & outer[None, :]
    parity = jnp.zeros((table_order, table_order), jnp.int32)
    for bit_pos in range(max((table_order // piece).bit_length() - 1, 0)):
        parity = parity + (common_bits >> bit_pos & 1)
    table = jnp.where(parity % 2 == 0, 1.0, -1.0).astype(jnp.float32)
    inner = counter % piece
    return jnp.where(inner[:, None] == inner[None, :], table, 0.0)


def dot_tt(a, b):
    return lax.dot_general(a, b, (((0,), (0,)), ((), ())), precision=exact_mode,
                           preferred_element_type=jnp.float32)


def dot_nn(a, b):
    return lax.dot_general(a, b, (((1,), (0,)), ((), ())), precision=exact_mode,
                           preferred_element_type=jnp.float32)


def factor_tile(block):
    groups = TILE // SUB
    lane = lax.broadcasted_iota(jnp.int32, (SUB, TILE), 1)
    sub = lax.broadcasted_iota(jnp.int32, (SUB, TILE), 0)
    left = [block[SUB * g:SUB * (g + 1), :] for g in range(groups)]
    right = [(lane == sub + SUB * g).astype(jnp.float32) for g in range(groups)]
    for j in range(TILE):
        g, s = divmod(j, SUB)
        inv = 1.0 / left[g][s:s + 1, j:j + 1]
        row = left[g][s:s + 1, :] * inv
        row_e = right[g][s:s + 1, :] * inv
        for h in range(g, groups):
            col = jnp.broadcast_to(left[h][:, j:j + 1], (SUB, TILE))
            if h == g:
                if s == SUB - 1:
                    continue
                col = jnp.where(sub > s, col, 0.0)
            left[h] = left[h] - col * row
            right[h] = right[h] - col * row_e
    for g in range(groups):
        pivot = jnp.sum(jnp.where(lane == sub + SUB * g, left[g], 0.0), axis=1, keepdims=True)
        root = jnp.sqrt(pivot)
        left[g] = jnp.where(lane >= sub + SUB * g, left[g] / root, 0.0)
        right[g] = jnp.where(lane <= sub + SUB * g, right[g] / root, 0.0)
    return jnp.concatenate(left, axis=0), jnp.concatenate(right, axis=0)


def factor_kernel(packed_ref, atb_ref, squares_ref, tri_ref, direction_ref, alpha_ref, work, inverse):
    n = tri_ref.shape[0]
    tiles = n // TILE
    offset = 0
    for i in range(tiles):
        for j in range(i, tiles):
            work[i * TILE:(i + 1) * TILE, j * TILE:(j + 1) * TILE] = packed_ref[offset:offset + TILE, :]
            offset += TILE
        if i:
            work[i * TILE:(i + 1) * TILE, :i * TILE] = jnp.zeros((TILE, i * TILE), jnp.float32)
    work[:, n:] = atb_ref[...]
    width = work.shape[1]

    def step(k, carry):
        at = pl.multiple_of(k * TILE, TILE)
        here = pl.ds(at, TILE)
        upper, inv = factor_tile(work[here, here])
        inverse[here, :] = inv
        column = lax.broadcasted_iota(jnp.int32, (TILE, width), 1)
        panel = dot_nn(inv, work[here, :])
        work[here, :] = jnp.where(column >= at + TILE, panel, 0.0)
        work[here, here] = upper

        def trail(i, carry):
            there = pl.ds(pl.multiple_of(i * TILE, TILE), TILE)
            work[there, :] = work[there, :] - dot_tt(work[here, there], work[here, :])
            return carry

        return lax.fori_loop(k + 1, tiles, trail, carry)

    lax.fori_loop(0, tiles, step, 0)
    tri_ref[...] = work[:, :n]
    beta = jnp.sqrt(squares_ref[0:1, :])
    lifted = work[:, n:] / beta
    alpha = jnp.sqrt(jnp.sum(lifted * lifted, axis=0, keepdims=True))
    alpha_ref[...] = jnp.broadcast_to(alpha, alpha_ref.shape)
    work[:, n:] = lifted / alpha
    direction_ref[...] = jnp.zeros_like(direction_ref)

    def back(t, carry):
        k = tiles - 1 - t
        here = pl.ds(pl.multiple_of(k * TILE, TILE), TILE)
        rest = work[here, n:] - dot_nn(tri_ref[here, :], direction_ref[...])
        direction_ref[here, :] = dot_tt(inverse[here, :], rest)
        return carry

    lax.fori_loop(0, tiles, back, 0)


def factor_and_solve(packed, atb, squares):
    n, k = atb.shape
    return pl.pallas_call(
        factor_kernel,
        out_shape=(
            jax.ShapeDtypeStruct((n, n), jnp.float32),
            jax.ShapeDtypeStruct((n, k), jnp.float32),
            jax.ShapeDtypeStruct((SUB, k), jnp.float32),
        ),
        in_specs=[pl.BlockSpec(memory_space=pltpu.VMEM)] * 3,
        out_specs=(pl.BlockSpec(memory_space=pltpu.VMEM),) * 3,
        scratch_shapes=[
            pltpu.VMEM((n, n + k), jnp.float32),
            pltpu.VMEM((n, TILE), jnp.float32),
        ],
        compiler_params=pltpu.CompilerParams(vmem_limit_bytes=48 * 1024 * 1024),
        name="factor_and_solve",
    )(packed, atb, squares)


def shards(mat, signs, picks, rhs):
    row_count, n = mat.shape
    devices = lax.axis_size("rows") * lax.axis_size("grp")
    samples = picks.shape[0] * devices
    piece = row_count // devices

    atb_part = dot_tt(mat, rhs)
    atb = lax.psum(atb_part, AXES)

    local_rows = lax.iota(jnp.int32, row_count)
    hits = jnp.sum(
        ((picks % row_count)[:, None] == local_rows[None, :]).astype(jnp.float32), axis=0
    ) * (1.0 / samples)
    squares_part = jnp.sum(rhs * rhs, axis=0, keepdims=True)
    small = jnp.concatenate(
        [
            jnp.broadcast_to(squares_part, (devices, rhs.shape[1])),
            hits.reshape(devices, piece),
        ],
        axis=1,
    )
    small = lax.all_to_all(small, AXES, 0, 0, tiled=True)
    hits = small[:, rhs.shape[1]:]
    squares = jnp.broadcast_to(
        jnp.sum(small[:, :rhs.shape[1]], axis=0, keepdims=True), (SUB, rhs.shape[1])
    )

    mixed = mat * signs.astype(jnp.float32)[:, None]
    mixed = dot_nn(walsh_table(row_count), mixed)
    if piece % SUB == 0:
        turned = lax.all_to_all(mixed, AXES, 0, 0, tiled=True)
    else:
        turned = mixed.reshape(devices, piece * n // TILE, TILE)
        turned = lax.all_to_all(turned, AXES, 0, 0, tiled=True).reshape(row_count, n)
    turned = dot_nn(walsh_table(row_count, piece), turned)
    weighted = turned * hits.reshape(row_count, 1)
    strips = [
        dot_tt(weighted[:, at:at + TILE], turned[:, at:]) for at in range(0, n, TILE)
    ]
    tiles = [
        strip[:, at:at + TILE] for strip in strips for at in range(0, strip.shape[1], TILE)
    ]
    packed = lax.psum(jnp.concatenate(tiles, axis=0), AXES)

    tri, direction, alpha = factor_and_solve(packed, atb, squares)
    alpha = alpha[0]
    beta = jnp.sqrt(squares[0])
    image = dot_nn(mat, direction)
    pushed = image - alpha / beta * rhs
    gamma_part = jnp.sum(pushed * pushed, axis=0, keepdims=True)
    gamma_parts = lax.all_to_all(
        jnp.broadcast_to(gamma_part, (devices, rhs.shape[1])), AXES, 0, 0, tiled=True
    )
    gamma_sq = jnp.sum(gamma_parts, axis=0)
    coef = beta * alpha / (alpha * alpha + gamma_sq)
    return (tri, direction * coef, rhs - image * coef)


def solution(mesh):
    return jax.shard_map(
        shards,
        mesh=mesh,
        in_specs=(P(AXES, None), P(AXES), P(AXES), P(AXES, None)),
        out_specs=(P(), P(), P(AXES, None)),
        check_vma=False,
    )
```
